32 devices in a mesh: ctx: 8 (over y, x, core), fsdp: 4 (over z).
Axes of the slice: x: 2, y: 2, z: 4, core: 2. Of those that a mesh axis runs over, the one named last changes fastest.
Arguments:
- xbc: bfloat16 [4, 1024, 9216], P('fsdp', 'ctx'), may hold values from -6 to 6
- dt_raw: bfloat16 [4, 128, 1024], P('fsdp', None, 'ctx'), may hold values from -4 to 15
- dy: bfloat16 [4, 1024, 8192], P('fsdp', 'ctx'), may hold values from -6 to 6
- conv_params: float32 [5, 9216], replicated, may hold values from -3 to 3
- head_params: float32 [3, 128], replicated, may hold values from -13 to 1.5, as said below
Outputs:
- d_xbc: bfloat16 [4, 1024, 9216], P('fsdp', 'ctx')
- d_dt_raw: float32 [4, 128, 1024], P('fsdp', None, 'ctx')
- d_conv: float32 [5, 9216], replicated
- d_head: float32 [3, 128], replicated
The draws below stay inside these ranges and needn't reach their ends.
Inputs may be any that keep to these rules, and one draw needn't show every extreme that they name: `head_params`: head parameters.
All inputs are finite; a program needn't handle non-finite values.
Results may differ from the reference program's by a relative error of at most 0.007.
Values may be sent and summed in bfloat16 or wider, within the bound.
A program may use at most 256 MiB of HBM per device.

```python
import jax
import jax.numpy as jnp
from jax import lax

HEADS = 128
HEAD_DIM = 64
STATE = 128
GROUPS = 4
CONV_W = 4
SPAN = 128
TOK_DEV = 128
SEQ_LEN = 1024
BATCH = 4
CHANNELS = 9216


def draw_head_params(key, part):
    keys = jax.random.split(jax.random.fold_in(key, 11), 5)
    share = 0.5
    fast_heads = jax.random.bernoulli(keys[0], share, (HEADS,))
    slow_level = jax.random.uniform(keys[1], (HEADS,), jnp.float32, 0.15, 0.4)
    slow_bias = jnp.log(slow_level / (SEQ_LEN * 1.0))
    fast_bias = jax.random.uniform(keys[2], (HEADS,), jnp.float32, -2.6, -1.9)
    spread_log = jax.random.uniform(keys[3], (HEADS,), jnp.float32, -0.5, 0.5)
    log_rate = jnp.where(fast_heads, jnp.log(0.25) + spread_log, spread_log)
    step_bias = jnp.where(fast_heads, fast_bias, slow_bias)
    skip_gain = jax.random.uniform(keys[4], (HEADS,), jnp.float32, 0.5, 1.5)
    return jnp.stack([step_bias, log_rate, skip_gain]).astype(jnp.float32)


def draw_dt_raw(key, part):
    keys = jax.random.split(jax.random.fold_in(key, 23), 4)
    shape_full = (BATCH, HEADS, SEQ_LEN)
    stochastic_perturbation = jnp.clip(0.8 * jax.random.normal(keys[0], shape_full, jnp.float32), -3.2, 3.2)
    segment = TOK_DEV // 2
    segment_count = SEQ_LEN // segment
    beginning_displacements = jax.random.uniform(keys[1], (BATCH, 1, segment_count), jnp.float32, -0.8, 0.8)
    beginning_displacements = jnp.repeat(beginning_displacements, segment, axis=2)
    drawn_locations = jax.random.randint(keys[2], (BATCH, 3), 0, SEQ_LEN)
    tier_magnitudes = jnp.log(SEQ_LEN * 1.0) + jax.random.uniform(keys[3], (BATCH, 3), jnp.float32, 0.0, 0.5)
    segment_positions = jnp.arange(SEQ_LEN)
    cluster_sets = jnp.sum(jnp.where(segment_positions[None, None, :] == drawn_locations[:, :, None], tier_magnitudes[:, :, None], 0.0), axis=1)
    overall_accumulation = jnp.clip(stochastic_perturbation + beginning_displacements + cluster_sets[:, None, :], -4.0, 15.0)
    return overall_accumulation.astype(jnp.bfloat16)


def level_of(stream_key, shape, cuts, least, top_value):
    factor_of, own = 1.0, jax.random.fold_in(stream_key, 6)
    for dim, parts in cuts:
        steps = jnp.exp(jax.random.uniform(jax.random.fold_in(own, dim), (parts,), jnp.float32, least / len(cuts), top_value / len(cuts)))
        factor_of = factor_of * jnp.repeat(steps, shape[dim] // parts).reshape([-1 if axis == dim else 1 for axis in range(len(shape))])
    return factor_of


def scatter_about(stream_key, dims, width, limit, cuts=(), kind=jnp.bfloat16):
    result = width * jax.random.normal(stream_key, dims, jnp.float32)
    if cuts:
        result = result * level_of(stream_key, dims, cuts, -0.22, 0.18)
    return jnp.clip(result, -limit, limit).astype(kind)


def setup_inputs(seed: int = 0) -> dict:
    arg_keys = jax.random.split(jax.random.key(seed), 6)
    xbc = scatter_about(arg_keys[0], (BATCH, SEQ_LEN, CHANNELS), 1.0, 6.0, ((0, 4), (1, 8)))
    dt_raw = draw_dt_raw(jax.random.fold_in(arg_keys[5], 71), 0)
    dy = scatter_about(arg_keys[2], (BATCH, SEQ_LEN, HEADS * HEAD_DIM), 1.0, 6.0, ((0, 4), (1, 8)))
    conv_params = scatter_about(arg_keys[3], (CONV_W + 1, CHANNELS), 0.5, 3.0, (), jnp.float32)
    head_params = draw_head_params(jax.random.fold_in(arg_keys[5], 71), 0)
    return dict(xbc=xbc, dt_raw=dt_raw, dy=dy, conv_params=conv_params, head_params=head_params)


exact_prec = lax.Precision.HIGHEST

def split_channels(activated):
    row_count = activated.shape[0]
    x_width = HEADS * HEAD_DIM
    bc_width = GROUPS * STATE
    x_heads = activated[:, :x_width].reshape(row_count, HEADS, HEAD_DIM)
    b_groups = activated[:, x_width:x_width + bc_width].reshape(row_count, GROUPS, STATE)
    c_groups = activated[:, x_width + bc_width:].reshape(row_count, GROUPS, STATE)
    return (x_heads, b_groups, c_groups)

def prepare(extended, dt_values, conv_params, head_params):
    row_count = extended.shape[0] - (CONV_W - 1)
    mixed_in = jnp.broadcast_to(conv_params[CONV_W][None, :], (row_count, extended.shape[1]))
    for offset in range(CONV_W):
        mixed_in = mixed_in + conv_params[offset][None, :] * extended[offset:offset + row_count]
    activated = jax.nn.silu(mixed_in)
    x_heads, b_groups, c_groups = split_channels(activated)
    step_size = jax.nn.softplus(dt_values + head_params[0][:, None])
    rates = step_size * jnp.exp(head_params[1])[:, None]
    return (x_heads, b_groups, c_groups, step_size, rates)

def span_outputs(x_heads, b_groups, c_groups, step_size, rates, head_params):
    row_count = x_heads.shape[0]
    block_count = row_count // SPAN
    per_group = HEADS // GROUPS
    x_blocks = x_heads.reshape(block_count, SPAN, HEADS, HEAD_DIM)
    b_blocks = b_groups.reshape(block_count, SPAN, GROUPS, STATE)
    c_blocks = c_groups.reshape(block_count, SPAN, GROUPS, STATE)
    d_blocks = step_size.reshape(HEADS, block_count, SPAN).transpose(1, 0, 2)
    l_blocks = rates.reshape(HEADS, block_count, SPAN).transpose(1, 0, 2)
    causal_mask = jnp.arange(SPAN)[:, None] >= jnp.arange(SPAN)[None, :]

    def advance(state_now, block):
        x_block, b_block, c_block, d_block, l_block = block
        running = jnp.cumsum(l_block, axis=1)
        spacing = jnp.where(causal_mask[None], running[:, :, None] - running[:, None, :], 0.0)
        fading = jnp.where(causal_mask[None], jnp.exp(-spacing), 0.0)
        scores = jnp.einsum('tgn,sgn->gts', c_block, b_block, precision=exact_prec)
        weights = scores[:, None] * fading.reshape(GROUPS, per_group, SPAN, SPAN) * d_block.reshape(GROUPS, per_group, 1, SPAN)
        x_grouped = x_block.reshape(SPAN, GROUPS, per_group, HEAD_DIM)
        outputs = jnp.einsum('gkts,sgkp->tgkp', weights, x_grouped, precision=exact_prec)
        carried = jnp.einsum('tgn,gkpn->tgkp', c_block, state_now.reshape(GROUPS, per_group, HEAD_DIM, STATE), precision=exact_prec)
        decay_rows = jnp.exp(-running).T.reshape(SPAN, GROUPS, per_group)[..., None]
        outputs = (outputs + carried * decay_rows).reshape(SPAN, HEADS, HEAD_DIM)
        tail_weight = (jnp.exp(running - running[:, -1:]) * d_block).T
        weighted = (tail_weight[:, :, None] * x_block).reshape(SPAN, GROUPS, per_group, HEAD_DIM)
        fresh_state = jnp.einsum('sgkp,sgn->gkpn', weighted, b_block, precision=exact_prec).reshape(HEADS, HEAD_DIM, STATE)
        state_next = jnp.exp(-running[:, -1])[:, None, None] * state_now + fresh_state
        return (state_next, outputs)
    initial = jnp.zeros((HEADS, HEAD_DIM, STATE), jnp.float32)
    _, outputs = lax.scan(advance, initial, (x_blocks, b_blocks, c_blocks, d_blocks, l_blocks))
    outputs = outputs.reshape(row_count, HEADS, HEAD_DIM) + head_params[2][None, :, None] * x_heads
    return outputs.reshape(row_count, HEADS * HEAD_DIM)

def sequence_grads(xbc_seq, dt_seq, dy_seq, conv_params, head_params):

    def forward(xbc_values, dt_values, conv_values, head_values):
        padding = jnp.zeros((CONV_W - 1, xbc_values.shape[1]), jnp.float32)
        extended = jnp.concatenate([padding, xbc_values], axis=0)
        pieces = prepare(extended, dt_values, conv_values, head_values)
        return span_outputs(*pieces, head_values)
    _, pullback = jax.vjp(forward, xbc_seq.astype(jnp.float32), dt_seq.astype(jnp.float32), conv_params, head_params)
    return pullback(dy_seq.astype(jnp.float32))

def reference(xbc, dt_raw, dy, conv_params, head_params):

    def per_sequence(sample):
        return sequence_grads(sample[0], sample[1], sample[2], conv_params, head_params)
    grad_x, grad_dt, grad_conv, grad_head = lax.map(per_sequence, (xbc, dt_raw, dy))
    return (grad_x.astype(jnp.bfloat16), grad_dt, lax.optimization_barrier(jnp.sum(grad_conv, axis=0)), lax.optimization_barrier(jnp.sum(grad_head, axis=0)))
```

```python
import functools

import jax
import jax.numpy as jnp
from jax import lax
from jax.experimental import pallas as pl
from jax.experimental.pallas import tpu as pltpu
from jax.sharding import PartitionSpec as P

HEADS = 128
HEAD_DIM = 64
STATE = 128
GROUPS = 4
CONV_W = 4
T = 128
LANES = 128
X_WIDTH = HEADS * HEAD_DIM
CHANNELS = X_WIDTH + 2 * GROUPS * STATE
PAIRS = HEADS // 2
PER_GROUP = PAIRS // GROUPS
F32 = jnp.float32
BF16 = jnp.bfloat16
MESH = pl.DeviceIdType.MESH
CHUNKS = 16
CHUNK_HEADS = HEADS // CHUNKS
CHUNK_ROWS = X_WIDTH // CHUNKS
LAG = 2
TAIL = 16
BLOCKS = CHANNELS // LANES


def dot(a, b, ca, cb, precision=None):
    return lax.dot_general(
        a, b, (((ca,), (cb,)), ((), ())), precision=precision, preferred_element_type=F32
    )


def block_of(i):
    return pl.ds(pl.multiple_of(i * LANES, LANES), LANES)


def sigmoid(v):
    return 1.0 / (1.0 + jnp.exp(-v))


def softplus(v):
    z = jnp.exp(-jnp.abs(v))
    small = z * (1.0 - z * (0.5 - z * (1.0 / 3.0 - z * 0.25)))
    return jnp.maximum(v, 0.0) + jnp.where(z < 0.01, small, jnp.log(1.0 + z))


def iota2(shape, dim):
    return lax.broadcasted_iota(jnp.int32, shape, dim)


def wide_pair(ht_ref, h):
    top = jnp.broadcast_to(ht_ref[pl.ds(h, 1), :], (HEAD_DIM, T))
    low = jnp.broadcast_to(ht_ref[pl.ds(h + 1, 1), :], (HEAD_DIM, T))
    return jnp.concatenate([top, low], axis=0).T


def states_kernel(
    xbc_ref, halo_ref, dt_ref, dy_ref, conv_ref, head_ref,
    mixed_ref, leave_ref, pull_ref, fade_ref, run_ref, step_ref, b_ref, c_ref,
    ext,
):
    step_th = softplus(dt_ref[...].astype(F32).T + head_ref[0:1, :])
    rate_th = step_th * jnp.exp(head_ref[1:2, :])
    lower = (iota2((T, T), 0) >= iota2((T, T), 1)).astype(F32)
    run_ht = dot(lower, rate_th, 1, 0, lax.Precision.HIGHEST).T
    run_ref[...] = run_ht
    step_ref[...] = step_th.T
    fade_ref[...] = jnp.broadcast_to(jnp.exp(-run_ht[:, T - 1 : T]), (HEADS, LANES))

    def convolve(i):
        cols = block_of(i)
        ext[0:8, :] = halo_ref[:, cols].astype(F32)
        ext[8 : 8 + T, :] = xbc_ref[:, cols].astype(F32)
        mixed = conv_ref[CONV_W : CONV_W + 1, cols] + conv_ref[0:1, cols] * ext[5 : 5 + T, :]
        for j in range(1, CONV_W):
            mixed = mixed + conv_ref[j : j + 1, cols] * ext[5 + j : 5 + j + T, :]
        mixed_ref[:, cols] = mixed
        return mixed * sigmoid(mixed)

    def bc(g, _):
        b_ref[:, block_of(g)] = convolve(PAIRS + g).astype(BF16)
        c_ref[:, block_of(g)] = convolve(PAIRS + GROUPS + g).astype(BF16)
        return 0

    lax.fori_loop(0, GROUPS, bc, 0)

    def pair(i, _):
        g = i // PER_GROUP
        x = convolve(i)
        run = wide_pair(run_ref, 2 * i)
        step = wide_pair(step_ref, 2 * i)
        tail = (x * step * jnp.exp(run - run[T - 1 : T, :])).astype(BF16)
        out = (jnp.exp(-run) * dy_ref[:, block_of(i)].astype(F32)).astype(BF16)
        leave_ref[block_of(i), :] = dot(tail, b_ref[:, block_of(g)], 0, 0)
        pull_ref[block_of(i), :] = dot(out, c_ref[:, block_of(g)], 0, 0)
        return 0

    lax.fori_loop(0, PAIRS, pair, 0)


def chain_kernel(count, leave_ref, pull_ref, fade_ref, enter_ref, later_ref,
                 out_f, out_b, in_f, in_b, send_f, recv_f, send_b, recv_b):
    me = lax.axis_index("ctx")
    barrier = pltpu.get_barrier_semaphore()
    first, last = me == 0, me == count - 1

    for peer in (lax.rem(me + 1, count), lax.rem(me + count - 1, count)):
        pl.semaphore_signal(barrier, inc=1, device_id={"ctx": peer}, device_id_type=MESH)
    pl.semaphore_wait(barrier, 2)

    def rows_of(c):
        return pl.ds(pl.multiple_of(c * CHUNK_ROWS, CHUNK_ROWS), CHUNK_ROWS)

    def copy(c, src, dst, send, recv, peer):
        return pltpu.make_async_remote_copy(
            src_ref=src.at[rows_of(c)], dst_ref=dst.at[rows_of(c)],
            send_sem=send.at[c], recv_sem=recv.at[c],
            device_id={"ctx": peer}, device_id_type=MESH,
        )

    def handle(c, own, src, dst, send, recv, peer, begins, ends, result):
        @pl.when(begins)
        def _():
            result[rows_of(c), :] = jnp.zeros((CHUNK_ROWS, LANES), BF16)

        @pl.when(jnp.logical_not(begins))
        def _():
            copy(c, src, dst, send, recv, peer).wait_recv()
            result[rows_of(c), :] = dst[rows_of(c), :]

        @pl.when(jnp.logical_not(ends))
        def _():
            for k in range(CHUNK_HEADS):
                rows = pl.ds(pl.multiple_of(c * CHUNK_ROWS + k * HEAD_DIM, HEAD_DIM), HEAD_DIM)
                fade = fade_ref[pl.ds(c * CHUNK_HEADS + k, 1), :]
                src[rows, :] = (fade * result[rows, :].astype(F32) + own[rows, :]).astype(BF16)
            copy(c, src, dst, send, recv, peer).start()

    up = jnp.minimum(me + 1, count - 1)
    down = jnp.maximum(me - 1, 0)

    def tick(v, _):
        c = v - me * LAG

        @pl.when(jnp.logical_and(c >= 0, c < CHUNKS))
        def _():
            handle(c, leave_ref, out_f, in_f, send_f, recv_f, up, first, last, enter_ref)

        d = v - (count - 1 - me) * LAG

        @pl.when(jnp.logical_and(d >= 0, d < CHUNKS))
        def _():
            handle(d, pull_ref, out_b, in_b, send_b, recv_b, down, last, first, later_ref)

        return 0

    lax.fori_loop(0, CHUNKS + (count - 1) * LAG, tick, 0)

    def drain(c, _):
        @pl.when(jnp.logical_not(last))
        def _():
            copy(c, out_f, in_f, send_f, recv_f, up).wait_send()

        @pl.when(jnp.logical_not(first))
        def _():
            copy(c, out_b, in_b, send_b, recv_b, down).wait_send()

        return 0

    lax.fori_loop(0, CHUNKS, drain, 0)


def grads_kernel(
    xbc_ref, halo_ref, dt_ref, dy_ref, conv_ref, head_ref,
    mixed_ref, run_ref, step_ref, b_ref, c_ref, enter_ref, later_ref,
    dx_ref, tail_ref, rim_ref, packed_ref, ddt_ref,
    ext, dms, skip_ref, scores, dscores, db, dc, acc,
):
    skip_ref[...] = jnp.broadcast_to(head_ref[2:3, :], (LANES, HEADS)).T
    acc[...] = jnp.zeros_like(acc)
    packed_ref[...] = jnp.zeros_like(packed_ref)
    dms[0:8, :] = jnp.zeros((8, LANES), F32)
    dms[8 + T : 16 + T, :] = jnp.zeros((8, LANES), F32)
    causal = iota2((T, T), 0) >= iota2((T, T), 1)
    lane = iota2((T, LANES), 1)
    left = lane < HEAD_DIM

    def conv_back(i, mixed, sig, dact):
        cols = block_of(i)
        dm = dact * (sig * (1.0 + mixed * (1.0 - sig)))
        dms[8 : 8 + T, :] = dm
        ext[0:8, :] = halo_ref[:, cols].astype(F32)
        ext[8 : 8 + T, :] = xbc_ref[:, cols].astype(F32)
        taps = [conv_ref[j : j + 1, cols] for j in range(CONV_W)]
        own = taps[3] * dm
        rim = taps[0] * dms[8:16, :]
        for j in range(3):
            own = own + taps[j] * dms[11 - j : 11 - j + T, :]
        for j in range(1, 3):
            rim = rim + taps[j] * dms[8 - j : 16 - j, :]
        dx_ref[:, cols] = own.astype(BF16)
        tail_ref[:, cols] = own[T - TAIL :, :]
        rim_ref[:, cols] = jnp.concatenate([rim, jnp.zeros_like(rim)], 0).astype(BF16)
        for j in range(CONV_W):
            packed_ref[i, j : j + 1, :] = jnp.sum(dm * ext[5 + j : 5 + j + T, :], 0, keepdims=True)
        packed_ref[i, CONV_W : CONV_W + 1, :] = jnp.sum(dm, 0, keepdims=True)

    def pair(i, g):
        h = 2 * i
        cols = block_of(i)
        mixed = mixed_ref[:, cols]
        sig = sigmoid(mixed)
        x = mixed * sig
        dy16 = dy_ref[:, cols]
        dy = dy16.astype(F32)
        step = wide_pair(step_ref, h)
        fades = []
        runs = []
        for k in range(2):
            row = jnp.broadcast_to(run_ref[pl.ds(h + k, 1), :], (T, T))
            col = row.T
            runs.append(col)
            fades.append(jnp.exp(jnp.where(causal, row - col, -1e30)))
        run = jnp.where(left, runs[0], runs[1])
        xd16 = (x * step).astype(BF16)
        xd = xd16.astype(F32)
        e_tail = jnp.exp(run - run[T - 1 : T, :])
        e_head = jnp.exp(-run)
        zero = jnp.zeros((T, LANES), BF16)
        bd_x = jnp.concatenate([jnp.where(left, xd16, zero), jnp.where(left, zero, xd16)], 0)
        bd_y = jnp.concatenate([jnp.where(left, dy16, zero), jnp.where(left, zero, dy16)], 0)
        sc = scores[...]
        w = [(sc * f).astype(BF16) for f in fades]
        enter = enter_ref[cols, :]
        later = later_ref[cols, :]
        b16 = b_ref[:, block_of(g)]
        c16 = c_ref[:, block_of(g)]
        y = dot(jnp.concatenate(w, 1), bd_x, 1, 0) + e_head * dot(c16, enter, 1, 1)
        from_tail = e_tail * dot(b16, later, 1, 1)
        dxd = dot(jnp.concatenate(w, 0), bd_y, 0, 0) + from_tail
        pairwise = dot(dy16, bd_x, 1, 1)
        dscores[...] += pairwise[:, :T] * fades[0] + pairwise[:, T:] * fades[1]
        dc[...] += dot((e_head * dy).astype(BF16), enter, 1, 0)
        db[...] += dot((xd * e_tail).astype(BF16), later, 1, 0)
        skip = jnp.where(left[0:1, :], skip_ref[pl.ds(h, 1), :], skip_ref[pl.ds(h + 1, 1), :])
        conv_back(i, mixed, sig, step * dxd + skip * dy)
        both = (enter.astype(F32) * later.astype(F32)).astype(BF16)
        passed = dot(jnp.ones((8, STATE), BF16), both, 1, 1)
        sub = iota2((8, LANES), 0)
        rows = jnp.where(sub == 0, jnp.sum(dy * x, 0, keepdims=True), 0.0)
        rows = rows + jnp.where(
            sub == 1,
            jnp.sum(xd * from_tail, 0, keepdims=True) + e_head[T - 1 : T, :] * passed[0:1, :],
            0.0,
        )
        value = jnp.concatenate([xd * dxd - dy * y, x * dxd, rows], 0)
        high = value.astype(BF16)
        low = (value - high.astype(F32)).astype(BF16)
        pick = (iota2((LANES, HEADS), 1) == h + iota2((LANES, HEADS), 0) // HEAD_DIM).astype(BF16)
        acc[...] += dot(
            jnp.concatenate([high, low], 1), jnp.concatenate([pick, pick], 0), 1, 0
        )

    def group(g, _):
        b16 = b_ref[:, block_of(g)]
        c16 = c_ref[:, block_of(g)]
        scores[...] = dot(c16, b16, 1, 1)
        dscores[...] = jnp.zeros_like(dscores)
        db[...] = jnp.zeros_like(db)
        dc[...] = jnp.zeros_like(dc)

        def inner(k, _):
            pair(g * PER_GROUP + k, g)
            return 0

        lax.fori_loop(0, PER_GROUP, inner, 0)
        ds = dscores[...].astype(BF16)
        for at, total in (
            (PAIRS + g, db[...] + dot(ds, c16, 0, 0)),
            (PAIRS + GROUPS + g, dc[...] + dot(ds, b16, 1, 0)),
        ):
            mixed = mixed_ref[:, block_of(at)]
            conv_back(at, mixed, sigmoid(mixed), total)
        return 0

    lax.fori_loop(0, GROUPS, group, 0)

    upper = (iota2((T, T), 0) <= iota2((T, T), 1)).astype(F32)
    d_rate = dot(upper, acc[0:T, :], 1, 0, lax.Precision.HIGHEST) - acc[2 * T + 1 : 2 * T + 2, :]
    scale = jnp.exp(head_ref[1:2, :])
    raw = dt_ref[...].astype(F32).T + head_ref[0:1, :]
    d_dt = (acc[T : 2 * T, :] + d_rate * scale) * sigmoid(raw)
    ddt_ref[...] = d_dt.T
    packed_ref[BLOCKS, 0:1, :] = jnp.sum(d_dt, 0, keepdims=True)
    packed_ref[BLOCKS, 1:2, :] = jnp.sum(d_rate * softplus(raw) * scale, 0, keepdims=True)
    packed_ref[BLOCKS, 2:3, :] = acc[2 * T : 2 * T + 1, :]


def sum_kernel(
    counts, packed_ref, tail_ref, rim_ref, conv_ref, head_ref, end_ref,
    parts, mine, planes, total, rim_in, send_a, recv_a, send_b, recv_b, send_c, recv_c, rim_sem,
):
    n, m = counts
    share = packed_ref.shape[0] // n
    me, plane = lax.axis_index("ctx"), lax.axis_index("fsdp")
    barrier = pltpu.get_barrier_semaphore()
    for r in range(1, n):
        peer = lax.rem(me + r, n)
        pl.semaphore_signal(barrier, inc=1, device_id={"ctx": peer}, device_id_type=MESH)
    for r in range(1, m):
        peer = lax.rem(plane + r, m)
        pl.semaphore_signal(barrier, inc=1, device_id={"fsdp": peer}, device_id_type=MESH)
    pl.semaphore_wait(barrier, n + m - 2)

    def piece(k):
        return pl.ds(k * share, share)

    def rim_copy():
        return pltpu.make_async_remote_copy(
            src_ref=rim_ref, dst_ref=rim_in, send_sem=rim_sem.at[0], recv_sem=rim_sem.at[1],
            device_id={"ctx": jnp.maximum(me - 1, 0)}, device_id_type=MESH,
        )

    def scatter(peer, slot):
        return pltpu.make_async_remote_copy(
            src_ref=packed_ref.at[piece(peer)], dst_ref=parts.at[slot],
            send_sem=send_a.at[peer], recv_sem=recv_a.at[slot],
            device_id={"ctx": peer}, device_id_type=MESH,
        )

    def across(peer, slot):
        return pltpu.make_async_remote_copy(
            src_ref=mine, dst_ref=planes.at[slot],
            send_sem=send_b.at[peer], recv_sem=recv_b.at[slot],
            device_id={"fsdp": peer}, device_id_type=MESH,
        )

    def gather(peer, slot):
        return pltpu.make_async_remote_copy(
            src_ref=total.at[piece(me)], dst_ref=total.at[piece(slot)],
            send_sem=send_c.at[peer], recv_sem=recv_c.at[slot],
            device_id={"ctx": peer}, device_id_type=MESH,
        )

    for r in range(1, n):
        scatter(lax.rem(me + r, n), me).start()

    @pl.when(me > 0)
    def _():
        rim_copy().start()

    parts[me] = packed_ref[piece(me)]
    for r in range(1, n):
        scatter(me, lax.rem(me + r, n)).wait_recv()
    own = parts[0]
    for k in range(1, n):
        own = own + parts[k]
    mine[...] = own
    for r in range(1, m):
        across(lax.rem(plane + r, m), plane).start()
    planes[plane] = own
    for r in range(1, m):
        across(plane, lax.rem(plane + r, m)).wait_recv()
    own = planes[0]
    for k in range(1, m):
        own = own + planes[k]
    total[piece(me)] = own
    for r in range(1, n):
        gather(lax.rem(me + r, n), me).start()

    @pl.when(me == n - 1)
    def _():
        end_ref[...] = tail_ref[...].astype(BF16)

    @pl.when(me < n - 1)
    def _():
        rim_copy().wait_recv()
        shift = TAIL - (CONV_W - 1)
        back = rim_in[...].astype(F32)
        pad = jnp.zeros((shift, CHANNELS), F32)
        moved = jnp.concatenate([pad, back[0 : CONV_W - 1, :]], 0)
        end_ref[...] = (tail_ref[...] + moved).astype(BF16)

    for r in range(1, n):
        gather(me, lax.rem(me + r, n)).wait_recv()
    for i in range(BLOCKS):
        conv_ref[:, i * LANES : (i + 1) * LANES] = total[i, 0 : CONV_W + 1, :]
    head_ref[...] = total[BLOCKS, 0:3, :]
    for r in range(1, n):
        scatter(lax.rem(me + r, n), me).wait_send()
        gather(lax.rem(me + r, n), me).wait_send()
    for r in range(1, m):
        across(lax.rem(plane + r, m), plane).wait_send()

    @pl.when(me > 0)
    def _():
        rim_copy().wait_send()


def vmem(count):
    return [pl.BlockSpec(memory_space=pltpu.VMEM)] * count


def call(kernel, out, scratch, args, limit=56, **params):
    return pl.pallas_call(
        kernel,
        out_shape=[jax.ShapeDtypeStruct(s, d) for s, d in out],
        in_specs=vmem(len(args)),
        out_specs=vmem(len(out)),
        scratch_shapes=scratch,
        compiler_params=pltpu.CompilerParams(vmem_limit_bytes=limit << 20, **params),
    )(*args)


def shifted(block, axis, distance):
    devices = range(lax.axis_size(axis))
    route = [(i - distance, i) for i in devices if i - distance in devices]
    return lax.ppermute(block, axis, route)


def shards(xbc, dt_raw, dy, conv_params, head_params):
    rim_rows = CONV_W - 1
    count = lax.axis_size("ctx")
    x = xbc[0]
    halo = jnp.pad(shifted(x[T - rim_rows :], "ctx", 1), ((8 - rim_rows, 0), (0, 0)))
    base = (x, halo, dt_raw[0], dy[0], conv_params, head_params)
    bc_width = GROUPS * STATE
    mixed, leave, pull, fade, run, step, b, c = call(
        states_kernel,
        [((T, CHANNELS), F32), ((X_WIDTH, STATE), F32), ((X_WIDTH, STATE), F32),
         ((HEADS, LANES), F32), ((HEADS, T), F32), ((HEADS, T), F32),
         ((T, bc_width), BF16), ((T, bc_width), BF16)],
        [pltpu.VMEM((8 + T, LANES), F32)],
        base,
    )
    wire = pltpu.VMEM((X_WIDTH, STATE), BF16)
    sems = pltpu.SemaphoreType.DMA((CHUNKS,))
    enter, later = call(
        functools.partial(chain_kernel, count),
        [((X_WIDTH, STATE), BF16)] * 2,
        [wire, wire, wire, wire, sems, sems, sems, sems],
        (leave, pull, fade),
        collective_id=0,
        has_side_effects=True,
    )
    planes = lax.axis_size("fsdp")
    share = pl.cdiv(BLOCKS + 1, count)
    dx, tail, rim, packed, ddt = call(
        grads_kernel,
        [((T, CHANNELS), BF16), ((TAIL, CHANNELS), F32), ((TAIL, CHANNELS), BF16),
         ((share * count, 8, LANES), F32), ((HEADS, T), F32)],
        [pltpu.VMEM((8 + T, LANES), F32), pltpu.VMEM((16 + T, LANES), F32),
         pltpu.VMEM((HEADS, LANES), F32), pltpu.VMEM((T, T), F32), pltpu.VMEM((T, T), F32),
         pltpu.VMEM((T, STATE), F32), pltpu.VMEM((T, STATE), F32),
         pltpu.VMEM((2 * T + 8, HEADS), F32)],
        (*base, mixed, run, step, b, c, enter, later),
    )
    piece = (share, 8, LANES)
    total_conv, total_head, end = call(
        functools.partial(sum_kernel, (count, planes)),
        [((CONV_W + 1, CHANNELS), F32), ((3, HEADS), F32), ((TAIL, CHANNELS), BF16)],
        [pltpu.VMEM((count, *piece), F32), pltpu.VMEM(piece, F32),
         pltpu.VMEM((planes, *piece), F32), pltpu.VMEM((share * count, 8, LANES), F32),
         pltpu.VMEM((TAIL, CHANNELS), BF16)]
        + [pltpu.SemaphoreType.DMA((k,)) for k in (count, count, planes, planes, count, count, 2)],
        (packed, tail, rim),
        collective_id=1,
        has_side_effects=True,
    )
    dx = lax.dynamic_update_slice(dx, end, (T - TAIL, 0))
    return (dx[None], ddt[None], total_conv, total_head)


def solution(mesh):
    return jax.shard_map(
        shards,
        mesh=mesh,
        in_specs=(P("fsdp", "ctx", None), P("fsdp", None, "ctx"), P("fsdp", "ctx", None), P(), P()),
        out_specs=(P("fsdp", "ctx", None), P("fsdp", None, "ctx"), P(), P()),
        check_vma=False,
    )
```

```python
import functools

import jax
import jax.numpy as jnp
from jax import lax
from jax.experimental import pallas as pl
from jax.experimental.pallas import tpu as pltpu
from jax.sharding import PartitionSpec as P

HEADS = 128
HEAD_DIM = 64
STATE = 128
GROUPS = 4
CONV_W = 4
T = 128
LANES = 128
X_WIDTH = HEADS * HEAD_DIM
CHANNELS = X_WIDTH + 2 * GROUPS * STATE
PAIRS = HEADS // 2
PER_GROUP = PAIRS // GROUPS
F32 = jnp.float32
BF16 = jnp.bfloat16
MESH = pl.DeviceIdType.MESH
CHUNKS = 16
CHUNK_HEADS = HEADS // CHUNKS
CHUNK_ROWS = X_WIDTH // CHUNKS
LAG = 2
TAIL = 16
BLOCKS = CHANNELS // LANES


def dot(a, b, ca, cb, precision=None):
    return lax.dot_general(
        a, b, (((ca,), (cb,)), ((), ())), precision=precision, preferred_element_type=F32
    )


def block_of(i):
    return pl.ds(pl.multiple_of(i * LANES, LANES), LANES)


def sigmoid(v):
    return 1.0 / (1.0 + jnp.exp(-v))


def softplus(v):
    z = jnp.exp(-jnp.abs(v))
    small = z * (1.0 - z * (0.5 - z * (1.0 / 3.0 - z * 0.25)))
    return jnp.maximum(v, 0.0) + jnp.where(z < 0.01, small, jnp.log(1.0 + z))


def iota2(shape, dim):
    return lax.broadcasted_iota(jnp.int32, shape, dim)


def wide_pair(ht_ref, h):
    top = jnp.broadcast_to(ht_ref[pl.ds(h, 1), :], (HEAD_DIM, T))
    low = jnp.broadcast_to(ht_ref[pl.ds(h + 1, 1), :], (HEAD_DIM, T))
    return jnp.concatenate([top, low], axis=0).T


def main_kernel(
    count,
    xbc_ref, halo_ref, dt_ref, dy_ref, conv_ref, head_ref,
    dx_ref, tail_ref, rim_ref, packed_ref, ddt_ref,
    ext, dms, mixed_ref, xd_ref, y_ref, dxd_ref, leave_ref, pull_ref,
    out_f, out_b, in_f, in_b, fade_ref, run_ref, step_ref, skip_ref, b_ref, c_ref,
    scores, dscores, db, dc, acc, send_f, recv_f, send_b, recv_b,
):
    me = lax.axis_index("ctx")
    barrier = pltpu.get_barrier_semaphore()
    first, last = me == 0, me == count - 1
    for peer in (lax.rem(me + 1, count), lax.rem(me + count - 1, count)):
        pl.semaphore_signal(barrier, inc=1, device_id={"ctx": peer}, device_id_type=MESH)

    step_th = softplus(dt_ref[...].astype(F32).T + head_ref[0:1, :])
    rate_th = step_th * jnp.exp(head_ref[1:2, :])
    lower = (iota2((T, T), 0) >= iota2((T, T), 1)).astype(F32)
    run_ht = dot(lower, rate_th, 1, 0, lax.Precision.HIGHEST).T
    run_ref[...] = run_ht
    step_ref[...] = step_th.T
    fade_ref[...] = jnp.broadcast_to(jnp.exp(-run_ht[:, T - 1 : T]), (HEADS, LANES))
    skip_ref[...] = jnp.broadcast_to(head_ref[2:3, :], (LANES, HEADS)).T
    acc[...] = jnp.zeros_like(acc)
    packed_ref[...] = jnp.zeros_like(packed_ref)
    dscores[...] = jnp.zeros_like(dscores)
    for slot in range(2):
        dms[slot, 0:8, :] = jnp.zeros((8, LANES), F32)
        dms[slot, 8 + T : 16 + T, :] = jnp.zeros((8, LANES), F32)
    causal = iota2((T, T), 0) >= iota2((T, T), 1)
    left = iota2((T, LANES), 1) < HEAD_DIM
    zero = jnp.zeros((T, LANES), BF16)

    def split(v):
        return jnp.concatenate([jnp.where(left, v, zero), jnp.where(left, zero, v)], 0)

    def convolve(i):
        cols = block_of(i)
        ext[0:8, cols] = halo_ref[:, cols].astype(F32)
        ext[8 : 8 + T, cols] = xbc_ref[:, cols].astype(F32)
        mixed = conv_ref[CONV_W : CONV_W + 1, cols] + conv_ref[0:1, cols] * ext[5 : 5 + T, cols]
        for j in range(1, CONV_W):
            mixed = mixed + conv_ref[j : j + 1, cols] * ext[5 + j : 5 + j + T, cols]
        mixed_ref[:, cols] = mixed
        return mixed * sigmoid(mixed)

    def bc(g, _):
        b16 = convolve(PAIRS + g).astype(BF16)
        c16 = convolve(PAIRS + GROUPS + g).astype(BF16)
        b_ref[:, block_of(g)] = b16
        c_ref[:, block_of(g)] = c16
        scores[g] = dot(c16, b16, 1, 1)
        return 0

    lax.fori_loop(0, GROUPS, bc, 0)

    def states(i):
        g = i // PER_GROUP
        x = convolve(i)
        run = wide_pair(run_ref, 2 * i)
        xd = (x * wide_pair(step_ref, 2 * i)).astype(BF16)
        xd_ref[:, block_of(i)] = xd
        tail = (xd.astype(F32) * jnp.exp(run - run[T - 1 : T, :])).astype(BF16)
        out = (jnp.exp(-run) * dy_ref[:, block_of(i)].astype(F32)).astype(BF16)
        leave_ref[block_of(i), :] = dot(tail, b_ref[:, block_of(g)], 0, 0)
        pull_ref[block_of(i), :] = dot(out, c_ref[:, block_of(g)], 0, 0)

    def states_two(k, _):
        states(2 * k)
        states(2 * k + 1)
        return 0

    lax.fori_loop(0, PAIRS // 2, states_two, 0)

    pl.semaphore_wait(barrier, 2)

    def rows_of(c):
        return pl.ds(pl.multiple_of(c * CHUNK_ROWS, CHUNK_ROWS), CHUNK_ROWS)

    def copy(c, src, dst, send, recv, peer):
        return pltpu.make_async_remote_copy(
            src_ref=src.at[rows_of(c)], dst_ref=dst.at[rows_of(c)],
            send_sem=send.at[c], recv_sem=recv.at[c],
            device_id={"ctx": peer}, device_id_type=MESH,
        )

    def handle(c, own, src, dst, send, recv, peer, begins, ends):
        @pl.when(begins)
        def _():
            dst[rows_of(c), :] = jnp.zeros((CHUNK_ROWS, LANES), BF16)

        @pl.when(jnp.logical_not(begins))
        def _():
            copy(c, src, dst, send, recv, peer).wait_recv()

        @pl.when(jnp.logical_not(ends))
        def _():
            for k in range(CHUNK_HEADS):
                rows = pl.ds(pl.multiple_of(c * CHUNK_ROWS + k * HEAD_DIM, HEAD_DIM), HEAD_DIM)
                fade = fade_ref[pl.ds(c * CHUNK_HEADS + k, 1), :]
                src[rows, :] = (fade * dst[rows, :].astype(F32) + own[rows, :]).astype(BF16)
            copy(c, src, dst, send, recv, peer).start()

    up = jnp.minimum(me + 1, count - 1)
    down = jnp.maximum(me - 1, 0)
    ticks = CHUNKS + (count - 1) * LAG
    load = pl.cdiv(PAIRS, ticks)

    def inner(i):
        h = 2 * i
        g = i // PER_GROUP
        cols = block_of(i)
        fades = []
        for k in range(2):
            row = jnp.broadcast_to(run_ref[pl.ds(h + k, 1), :], (T, T))
            fades.append(jnp.exp(jnp.where(causal, row - row.T, -1e30)))
        dy16 = dy_ref[:, cols]
        bd_x = split(xd_ref[:, cols])
        sc = scores[g]
        w = [(sc * f).astype(BF16) for f in fades]
        y_ref[:, cols] = dot(jnp.concatenate(w, 1), bd_x, 1, 0)
        dxd_ref[:, cols] = dot(jnp.concatenate(w, 0), split(dy16), 0, 0)
        pairwise = dot(dy16, bd_x, 1, 1)
        dscores[g] += pairwise[:, :T] * fades[0] + pairwise[:, T:] * fades[1]

    def tick(v, _):
        c = v - me * LAG

        @pl.when(jnp.logical_and(c >= 0, c < CHUNKS))
        def _():
            handle(c, leave_ref, out_f, in_f, send_f, recv_f, up, first, last)

        d = v - (count - 1 - me) * LAG

        @pl.when(jnp.logical_and(d >= 0, d < CHUNKS))
        def _():
            handle(d, pull_ref, out_b, in_b, send_b, recv_b, down, last, first)

        @pl.when((v + 1) * load <= PAIRS)
        def _():
            for k in range(load):
                inner(v * load + k)

        return 0

    lax.fori_loop(0, ticks, tick, 0)
    for i in range(PAIRS // load * load, PAIRS):
        inner(i)

    def conv_back(i, slot, mixed, sig, dact):
        cols = block_of(i)
        dm = dact * (sig * (1.0 + mixed * (1.0 - sig)))
        dms[slot, 8 : 8 + T, :] = dm
        taps = [conv_ref[j : j + 1, cols] for j in range(CONV_W)]
        own = taps[3] * dm
        rim = taps[0] * dms[slot, 8:16, :]
        for j in range(3):
            own = own + taps[j] * dms[slot, 11 - j : 11 - j + T, :]
        for j in range(1, 3):
            rim = rim + taps[j] * dms[slot, 8 - j : 16 - j, :]
        dx_ref[:, cols] = own.astype(BF16)
        tail_ref[:, cols] = own[T - TAIL :, :]
        rim_ref[:, cols] = jnp.concatenate([rim, jnp.zeros_like(rim)], 0).astype(BF16)
        for j in range(CONV_W):
            packed_ref[i, j : j + 1, :] = jnp.sum(
                dm * ext[5 + j : 5 + j + T, cols], 0, keepdims=True
            )
        packed_ref[i, CONV_W : CONV_W + 1, :] = jnp.sum(dm, 0, keepdims=True)

    def pair(i, g, slot):
        h = 2 * i
        cols = block_of(i)
        mixed = mixed_ref[:, cols]
        sig = sigmoid(mixed)
        x = mixed * sig
        dy = dy_ref[:, cols].astype(F32)
        step = wide_pair(step_ref, h)
        run = wide_pair(run_ref, h)
        xd = xd_ref[:, cols].astype(F32)
        e_tail = jnp.exp(run - run[T - 1 : T, :])
        e_head = jnp.exp(-run)
        enter = in_f[cols, :]
        later = in_b[cols, :]
        y = y_ref[:, cols] + e_head * dot(c_ref[:, block_of(g)], enter, 1, 1)
        from_tail = e_tail * dot(b_ref[:, block_of(g)], later, 1, 1)
        dxd = dxd_ref[:, cols] + from_tail
        dc[...] += dot((e_head * dy).astype(BF16), enter, 1, 0)
        db[...] += dot((xd * e_tail).astype(BF16), later, 1, 0)
        skip = jnp.where(left[0:1, :], skip_ref[pl.ds(h, 1), :], skip_ref[pl.ds(h + 1, 1), :])
        conv_back(i, slot, mixed, sig, step * dxd + skip * dy)
        both = (enter.astype(F32) * later.astype(F32)).astype(BF16)
        passed = dot(jnp.ones((8, STATE), BF16), both, 1, 1)
        sub = iota2((8, LANES), 0)
        rows = jnp.where(sub == 0, jnp.sum(dy * x, 0, keepdims=True), 0.0)
        rows = rows + jnp.where(
            sub == 1,
            jnp.sum(xd * from_tail, 0, keepdims=True) + e_head[T - 1 : T, :] * passed[0:1, :],
            0.0,
        )
        value = jnp.concatenate([xd * dxd - dy * y, x * dxd, rows], 0)
        high = value.astype(BF16)
        low = (value - high.astype(F32)).astype(BF16)
        pick = (iota2((LANES, HEADS), 1) == h + iota2((LANES, HEADS), 0) // HEAD_DIM).astype(BF16)
        acc[...] += dot(
            jnp.concatenate([high, low], 1), jnp.concatenate([pick, pick], 0), 1, 0
        )

    def group(g, _):
        db[...] = jnp.zeros_like(db)
        dc[...] = jnp.zeros_like(dc)

        def two(k, _):
            pair(g * PER_GROUP + 2 * k, g, 0)
            pair(g * PER_GROUP + 2 * k + 1, g, 1)
            return 0

        lax.fori_loop(0, PER_GROUP // 2, two, 0)
        ds = dscores[g].astype(BF16)
        b16 = b_ref[:, block_of(g)]
        c16 = c_ref[:, block_of(g)]
        for slot, at, total in (
            (0, PAIRS + g, db[...] + dot(ds, c16, 0, 0)),
            (1, PAIRS + GROUPS + g, dc[...] + dot(ds, b16, 1, 0)),
        ):
            mixed = mixed_ref[:, block_of(at)]
            conv_back(at, slot, mixed, sigmoid(mixed), total)
        return 0

    lax.fori_loop(0, GROUPS, group, 0)

    upper = (iota2((T, T), 0) <= iota2((T, T), 1)).astype(F32)
    d_rate = dot(upper, acc[0:T, :], 1, 0, lax.Precision.HIGHEST) - acc[2 * T + 1 : 2 * T + 2, :]
    scale = jnp.exp(head_ref[1:2, :])
    raw = dt_ref[...].astype(F32).T + head_ref[0:1, :]
    d_dt = (acc[T : 2 * T, :] + d_rate * scale) * sigmoid(raw)
    ddt_ref[...] = d_dt.T
    packed_ref[BLOCKS, 0:1, :] = jnp.sum(d_dt, 0, keepdims=True)
    packed_ref[BLOCKS, 1:2, :] = jnp.sum(d_rate * softplus(raw) * scale, 0, keepdims=True)
    packed_ref[BLOCKS, 2:3, :] = acc[2 * T : 2 * T + 1, :]

    def drain(c, _):
        @pl.when(jnp.logical_not(last))
        def _():
            copy(c, out_f, in_f, send_f, recv_f, up).wait_send()

        @pl.when(jnp.logical_not(first))
        def _():
            copy(c, out_b, in_b, send_b, recv_b, down).wait_send()

        return 0

    lax.fori_loop(0, CHUNKS, drain, 0)


def sum_kernel(
    counts, packed_ref, tail_ref, rim_ref, conv_ref, head_ref, end_ref,
    parts, mine, planes, total, rim_in, send_a, recv_a, send_b, recv_b, send_c, recv_c, rim_sem,
):
    n, m = counts
    share = packed_ref.shape[0] // n
    me, plane = lax.axis_index("ctx"), lax.axis_index("fsdp")
    barrier = pltpu.get_barrier_semaphore()
    for r in range(1, n):
        peer = lax.rem(me + r, n)
        pl.semaphore_signal(barrier, inc=1, device_id={"ctx": peer}, device_id_type=MESH)
    for r in range(1, m):
        peer = lax.rem(plane + r, m)
        pl.semaphore_signal(barrier, inc=1, device_id={"fsdp": peer}, device_id_type=MESH)
    pl.semaphore_wait(barrier, n + m - 2)

    def piece(k):
        return pl.ds(k * share, share)

    def rim_copy():
        return pltpu.make_async_remote_copy(
            src_ref=rim_ref, dst_ref=rim_in, send_sem=rim_sem.at[0], recv_sem=rim_sem.at[1],
            device_id={"ctx": jnp.maximum(me - 1, 0)}, device_id_type=MESH,
        )

    def scatter(peer, slot):
        return pltpu.make_async_remote_copy(
            src_ref=packed_ref.at[piece(peer)], dst_ref=parts.at[slot],
            send_sem=send_a.at[peer], recv_sem=recv_a.at[slot],
            device_id={"ctx": peer}, device_id_type=MESH,
        )

    def across(peer, slot):
        return pltpu.make_async_remote_copy(
            src_ref=mine, dst_ref=planes.at[slot],
            send_sem=send_b.at[peer], recv_sem=recv_b.at[slot],
            device_id={"fsdp": peer}, device_id_type=MESH,
        )

    def gather(peer, slot):
        return pltpu.make_async_remote_copy(
            src_ref=total.at[piece(me)], dst_ref=total.at[piece(slot)],
            send_sem=send_c.at[peer], recv_sem=recv_c.at[slot],
            device_id={"ctx": peer}, device_id_type=MESH,
        )

    for r in range(1, n):
        scatter(lax.rem(me + r, n), me).start()

    @pl.when(me > 0)
    def _():
        rim_copy().start()

    parts[me] = packed_ref[piece(me)]
    for r in range(1, n):
        scatter(me, lax.rem(me + r, n)).wait_recv()
    own = parts[0]
    for k in range(1, n):
        own = own + parts[k]
    mine[...] = own
    for r in range(1, m):
        across(lax.rem(plane + r, m), plane).start()
    planes[plane] = own
    for r in range(1, m):
        across(plane, lax.rem(plane + r, m)).wait_recv()
    own = planes[0]
    for k in range(1, m):
        own = own + planes[k]
    total[piece(me)] = own
    for r in range(1, n):
        gather(lax.rem(me + r, n), me).start()

    @pl.when(me == n - 1)
    def _():
        end_ref[...] = tail_ref[...].astype(BF16)

    @pl.when(me < n - 1)
    def _():
        rim_copy().wait_recv()
        shift = TAIL - (CONV_W - 1)
        back = rim_in[...].astype(F32)
        pad = jnp.zeros((shift, CHANNELS), F32)
        moved = jnp.concatenate([pad, back[0 : CONV_W - 1, :]], 0)
        end_ref[...] = (tail_ref[...] + moved).astype(BF16)

    for r in range(1, n):
        gather(me, lax.rem(me + r, n)).wait_recv()
    for i in range(BLOCKS):
        conv_ref[:, i * LANES : (i + 1) * LANES] = total[i, 0 : CONV_W + 1, :]
    head_ref[...] = total[BLOCKS, 0:3, :]
    for r in range(1, n):
        scatter(lax.rem(me + r, n), me).wait_send()
        gather(lax.rem(me + r, n), me).wait_send()
    for r in range(1, m):
        across(lax.rem(plane + r, m), plane).wait_send()

    @pl.when(me > 0)
    def _():
        rim_copy().wait_send()


def vmem(count):
    return [pl.BlockSpec(memory_space=pltpu.VMEM)] * count


def call(kernel, out, scratch, args, limit=56, **params):
    return pl.pallas_call(
        kernel,
        out_shape=[jax.ShapeDtypeStruct(s, d) for s, d in out],
        in_specs=vmem(len(args)),
        out_specs=vmem(len(out)),
        scratch_shapes=scratch,
        compiler_params=pltpu.CompilerParams(vmem_limit_bytes=limit << 20, **params),
    )(*args)


def shifted(block, axis, distance):
    devices = range(lax.axis_size(axis))
    route = [(i - distance, i) for i in devices if i - distance in devices]
    return lax.ppermute(block, axis, route)


def shards(xbc, dt_raw, dy, conv_params, head_params):
    rim_rows = CONV_W - 1
    count = lax.axis_size("ctx")
    x = xbc[0]
    halo = jnp.pad(shifted(x[T - rim_rows :], "ctx", 1), ((8 - rim_rows, 0), (0, 0)))
    base = (x, halo, dt_raw[0], dy[0], conv_params, head_params)
    planes = lax.axis_size("fsdp")
    share = pl.cdiv(BLOCKS + 1, count)
    wide, wide16 = pltpu.VMEM((T, X_WIDTH), F32), pltpu.VMEM((T, X_WIDTH), BF16)
    tall, tall16 = pltpu.VMEM((X_WIDTH, STATE), F32), pltpu.VMEM((X_WIDTH, STATE), BF16)
    small = pltpu.VMEM((T, LANES), F32)
    narrow = pltpu.VMEM((T, GROUPS * STATE), BF16)
    square = pltpu.VMEM((GROUPS, T, T), F32)
    dx, tail, rim, packed, ddt = call(
        functools.partial(main_kernel, count),
        [((T, CHANNELS), BF16), ((TAIL, CHANNELS), F32), ((TAIL, CHANNELS), BF16),
         ((share * count, 8, LANES), F32), ((HEADS, T), F32)],
        [pltpu.VMEM((8 + T, CHANNELS), F32), pltpu.VMEM((2, 16 + T, LANES), F32),
         pltpu.VMEM((T, CHANNELS), F32), wide16, wide, wide, tall, tall,
         tall16, tall16, tall16, tall16, small, small, small, small, narrow, narrow,
         square, square, small, small, pltpu.VMEM((2 * T + 8, HEADS), F32)]
        + [pltpu.SemaphoreType.DMA((CHUNKS,))] * 4,
        base,
        limit=60,
        collective_id=0,
        has_side_effects=True,
    )
    piece = (share, 8, LANES)
    total_conv, total_head, end = call(
        functools.partial(sum_kernel, (count, planes)),
        [((CONV_W + 1, CHANNELS), F32), ((3, HEADS), F32), ((TAIL, CHANNELS), BF16)],
        [pltpu.VMEM((count, *piece), F32), pltpu.VMEM(piece, F32),
         pltpu.VMEM((planes, *piece), F32), pltpu.VMEM((share * count, 8, LANES), F32),
         pltpu.VMEM((TAIL, CHANNELS), BF16)]
        + [pltpu.SemaphoreType.DMA((k,)) for k in (count, count, planes, planes, count, count, 2)],
        (packed, tail, rim),
        collective_id=1,
        has_side_effects=True,
    )
    dx = lax.dynamic_update_slice(dx, end, (T - TAIL, 0))
    return (dx[None], ddt[None], total_conv, total_head)


def solution(mesh):
    return jax.shard_map(
        shards,
        mesh=mesh,
        in_specs=(P("fsdp", "ctx", None), P("fsdp", None, "ctx"), P("fsdp", "ctx", None), P(), P()),
        out_specs=(P("fsdp", "ctx", None), P("fsdp", None, "ctx"), P(), P()),
        check_vma=False,
    )
```

```python
import functools

import jax
import jax.numpy as jnp
from jax import lax
from jax.experimental import pallas as pl
from jax.experimental.pallas import tpu as pltpu
from jax.sharding import PartitionSpec as P

HEADS = 128
HEAD_DIM = 64
STATE = 128
GROUPS = 4
CONV_W = 4
T = 128
LANES = 128
X_WIDTH = HEADS * HEAD_DIM
CHANNELS = X_WIDTH + 2 * GROUPS * STATE
PAIRS = HEADS // 2
PER_GROUP = PAIRS // GROUPS
F32 = jnp.float32
BF16 = jnp.bfloat16
MESH = pl.DeviceIdType.MESH
CHUNKS = 32
CHUNK_HEADS = HEADS // CHUNKS
CHUNK_ROWS = X_WIDTH // CHUNKS
LAG = 3
TAIL = 16
BLOCKS = CHANNELS // LANES


def dot(a, b, ca, cb, precision=None):
    return lax.dot_general(
        a, b, (((ca,), (cb,)), ((), ())), precision=precision, preferred_element_type=F32
    )


def block_of(i):
    return pl.ds(pl.multiple_of(i * LANES, LANES), LANES)


def sigmoid(v):
    return 1.0 / (1.0 + jnp.exp(-v))


def softplus(v):
    z = jnp.exp(-jnp.abs(v))
    small = z * (1.0 - z * (0.5 - z * (1.0 / 3.0 - z * 0.25)))
    return jnp.maximum(v, 0.0) + jnp.where(z < 0.01, small, jnp.log(1.0 + z))


def iota2(shape, dim):
    return lax.broadcasted_iota(jnp.int32, shape, dim)


def wide_pair(ht_ref, h):
    top = jnp.broadcast_to(ht_ref[pl.ds(h, 1), :], (HEAD_DIM, T))
    low = jnp.broadcast_to(ht_ref[pl.ds(h + 1, 1), :], (HEAD_DIM, T))
    return jnp.concatenate([top, low], axis=0).T


def main_kernel(
    count,
    xbc_ref, halo_ref, dt_ref, dy_ref, conv_ref, head_ref,
    dx_ref, tail_ref, rim_ref, packed_ref, ddt_ref,
    ext, dms, mixed_ref, xd_ref, y_ref, dxd_ref, leave_ref, pull_ref,
    out_f, out_b, in_f, in_b, fade_ref, run_ref, step_ref, skip_ref, b_ref, c_ref,
    scores, dscores, db, dc, acc, send_f, recv_f, send_b, recv_b,
):
    me = lax.axis_index("ctx")
    barrier = pltpu.get_barrier_semaphore()
    first, last = me == 0, me == count - 1
    for peer in (lax.rem(me + 1, count), lax.rem(me + count - 1, count)):
        pl.semaphore_signal(barrier, inc=1, device_id={"ctx": peer}, device_id_type=MESH)

    step_th = softplus(dt_ref[...].astype(F32).T + head_ref[0:1, :])
    rate_th = step_th * jnp.exp(head_ref[1:2, :])
    lower = (iota2((T, T), 0) >= iota2((T, T), 1)).astype(F32)
    run_ht = dot(lower, rate_th, 1, 0, lax.Precision.HIGHEST).T
    run_ref[...] = run_ht
    step_ref[...] = step_th.T
    fade_ref[...] = jnp.broadcast_to(jnp.exp(-run_ht[:, T - 1 : T]), (HEADS, LANES))
    skip_ref[...] = jnp.broadcast_to(head_ref[2:3, :], (LANES, HEADS)).T
    acc[...] = jnp.zeros_like(acc)
    packed_ref[...] = jnp.zeros_like(packed_ref)
    dscores[...] = jnp.zeros_like(dscores)
    for slot in range(2):
        dms[slot, 0:8, :] = jnp.zeros((8, LANES), F32)
        dms[slot, 8 + T : 16 + T, :] = jnp.zeros((8, LANES), F32)
    causal = iota2((T, T), 0) >= iota2((T, T), 1)
    left = iota2((T, LANES), 1) < HEAD_DIM
    zero = jnp.zeros((T, LANES), BF16)

    def split(v):
        return jnp.concatenate([jnp.where(left, v, zero), jnp.where(left, zero, v)], 0)

    def convolve(i):
        cols = block_of(i)
        ext[0:8, cols] = halo_ref[:, cols].astype(F32)
        ext[8 : 8 + T, cols] = xbc_ref[:, cols].astype(F32)
        mixed = conv_ref[CONV_W : CONV_W + 1, cols] + conv_ref[0:1, cols] * ext[5 : 5 + T, cols]
        for j in range(1, CONV_W):
            mixed = mixed + conv_ref[j : j + 1, cols] * ext[5 + j : 5 + j + T, cols]
        mixed_ref[:, cols] = mixed
        return mixed * sigmoid(mixed)

    def bc(g, _):
        b16 = convolve(PAIRS + g).astype(BF16)
        c16 = convolve(PAIRS + GROUPS + g).astype(BF16)
        b_ref[:, block_of(g)] = b16
        c_ref[:, block_of(g)] = c16
        scores[g] = dot(c16, b16, 1, 1)
        return 0

    lax.fori_loop(0, GROUPS, bc, 0)

    def states(i):
        g = i // PER_GROUP
        x = convolve(i)
        run = wide_pair(run_ref, 2 * i)
        xd = (x * wide_pair(step_ref, 2 * i)).astype(BF16)
        xd_ref[:, block_of(i)] = xd
        tail = (xd.astype(F32) * jnp.exp(run - run[T - 1 : T, :])).astype(BF16)
        out = (jnp.exp(-run) * dy_ref[:, block_of(i)].astype(F32)).astype(BF16)
        leave_ref[block_of(i), :] = dot(tail, b_ref[:, block_of(g)], 0, 0)
        pull_ref[block_of(i), :] = dot(out, c_ref[:, block_of(g)], 0, 0)

    pl.semaphore_wait(barrier, 2)

    def rows_of(c):
        return pl.ds(pl.multiple_of(c * CHUNK_ROWS, CHUNK_ROWS), CHUNK_ROWS)

    def copy(c, src, dst, send, recv, peer):
        return pltpu.make_async_remote_copy(
            src_ref=src.at[rows_of(c)], dst_ref=dst.at[rows_of(c)],
            send_sem=send.at[c], recv_sem=recv.at[c],
            device_id={"ctx": peer}, device_id_type=MESH,
        )

    def handle(c, own, src, dst, send, recv, peer, begins, ends):
        @pl.when(begins)
        def _():
            dst[rows_of(c), :] = jnp.zeros((CHUNK_ROWS, LANES), BF16)

        @pl.when(jnp.logical_not(begins))
        def _():
            copy(c, src, dst, send, recv, peer).wait_recv()

        @pl.when(jnp.logical_not(ends))
        def _():
            for k in range(CHUNK_HEADS):
                rows = pl.ds(pl.multiple_of(c * CHUNK_ROWS + k * HEAD_DIM, HEAD_DIM), HEAD_DIM)
                fade = fade_ref[pl.ds(c * CHUNK_HEADS + k, 1), :]
                src[rows, :] = (fade * dst[rows, :].astype(F32) + own[rows, :]).astype(BF16)
            copy(c, src, dst, send, recv, peer).start()

    up = jnp.minimum(me + 1, count - 1)
    down = jnp.maximum(me - 1, 0)
    ticks = CHUNKS + (count - 1) * LAG
    later_ticks = ticks - CHUNKS
    load = pl.cdiv(PAIRS, later_ticks)
    per_chunk = PAIRS // CHUNKS

    def inner(i):
        h = 2 * i
        g = i // PER_GROUP
        cols = block_of(i)
        fades = []
        for k in range(2):
            row = jnp.broadcast_to(run_ref[pl.ds(h + k, 1), :], (T, T))
            fades.append(jnp.exp(jnp.where(causal, row - row.T, -1e30)))
        dy16 = dy_ref[:, cols]
        bd_x = split(xd_ref[:, cols])
        sc = scores[g]
        w = [(sc * f).astype(BF16) for f in fades]
        y_ref[:, cols] = dot(jnp.concatenate(w, 1), bd_x, 1, 0)
        dxd_ref[:, cols] = dot(jnp.concatenate(w, 0), split(dy16), 0, 0)
        pairwise = dot(dy16, bd_x, 1, 1)
        dscores[g] += pairwise[:, :T] * fades[0] + pairwise[:, T:] * fades[1]

    def tick(v, _):
        @pl.when(v < CHUNKS)
        def _():
            for k in range(per_chunk):
                states(v * per_chunk + k)

        c = v - me * LAG

        @pl.when(jnp.logical_and(c >= 0, c < CHUNKS))
        def _():
            handle(c, leave_ref, out_f, in_f, send_f, recv_f, up, first, last)

        d = v - (count - 1 - me) * LAG

        @pl.when(jnp.logical_and(d >= 0, d < CHUNKS))
        def _():
            handle(d, pull_ref, out_b, in_b, send_b, recv_b, down, last, first)

        w = v - CHUNKS

        @pl.when(jnp.logical_and(w >= 0, (w + 1) * load <= PAIRS))
        def _():
            for k in range(load):
                inner(w * load + k)

        return 0

    lax.fori_loop(0, ticks, tick, 0)
    for i in range(PAIRS // load * load, PAIRS):
        inner(i)

    def conv_back(i, slot, mixed, sig, dact):
        cols = block_of(i)
        dm = dact * (sig * (1.0 + mixed * (1.0 - sig)))
        dms[slot, 8 : 8 + T, :] = dm
        taps = [conv_ref[j : j + 1, cols] for j in range(CONV_W)]
        own = taps[3] * dm
        rim = taps[0] * dms[slot, 8:16, :]
        for j in range(3):
            own = own + taps[j] * dms[slot, 11 - j : 11 - j + T, :]
        for j in range(1, 3):
            rim = rim + taps[j] * dms[slot, 8 - j : 16 - j, :]
        dx_ref[:, cols] = own.astype(BF16)
        tail_ref[:, cols] = own[T - TAIL :, :]
        rim_ref[:, cols] = jnp.concatenate([rim, jnp.zeros_like(rim)], 0).astype(BF16)
        for j in range(CONV_W):
            packed_ref[i, j : j + 1, :] = jnp.sum(
                dm * ext[5 + j : 5 + j + T, cols], 0, keepdims=True
            )
        packed_ref[i, CONV_W : CONV_W + 1, :] = jnp.sum(dm, 0, keepdims=True)

    def pair(i, g, slot):
        h = 2 * i
        cols = block_of(i)
        mixed = mixed_ref[:, cols]
        sig = sigmoid(mixed)
        x = mixed * sig
        dy = dy_ref[:, cols].astype(F32)
        step = wide_pair(step_ref, h)
        run = wide_pair(run_ref, h)
        xd = xd_ref[:, cols].astype(F32)
        e_tail = jnp.exp(run - run[T - 1 : T, :])
        e_head = jnp.exp(-run)
        enter = in_f[cols, :]
        later = in_b[cols, :]
        y = y_ref[:, cols] + e_head * dot(c_ref[:, block_of(g)], enter, 1, 1)
        from_tail = e_tail * dot(b_ref[:, block_of(g)], later, 1, 1)
        dxd = dxd_ref[:, cols] + from_tail
        dc[...] += dot((e_head * dy).astype(BF16), enter, 1, 0)
        db[...] += dot((xd * e_tail).astype(BF16), later, 1, 0)
        skip = jnp.where(left[0:1, :], skip_ref[pl.ds(h, 1), :], skip_ref[pl.ds(h + 1, 1), :])
        conv_back(i, slot, mixed, sig, step * dxd + skip * dy)
        both = (enter.astype(F32) * later.astype(F32)).astype(BF16)
        passed = dot(jnp.ones((8, STATE), BF16), both, 1, 1)
        sub = iota2((8, LANES), 0)
        rows = jnp.where(sub == 0, jnp.sum(dy * x, 0, keepdims=True), 0.0)
        rows = rows + jnp.where(
            sub == 1,
            jnp.sum(xd * from_tail, 0, keepdims=True) + e_head[T - 1 : T, :] * passed[0:1, :],
            0.0,
        )
        value = jnp.concatenate([xd * dxd - dy * y, x * dxd, rows], 0)
        high = value.astype(BF16)
        low = (value - high.astype(F32)).astype(BF16)
        pick = (iota2((LANES, HEADS), 1) == h + iota2((LANES, HEADS), 0) // HEAD_DIM).astype(BF16)
        acc[...] += dot(
            jnp.concatenate([high, low], 1), jnp.concatenate([pick, pick], 0), 1, 0
        )

    def group(g, _):
        db[...] = jnp.zeros_like(db)
        dc[...] = jnp.zeros_like(dc)

        def two(k, _):
            pair(g * PER_GROUP + 2 * k, g, 0)
            pair(g * PER_GROUP + 2 * k + 1, g, 1)
            return 0

        lax.fori_loop(0, PER_GROUP // 2, two, 0)
        ds = dscores[g].astype(BF16)
        b16 = b_ref[:, block_of(g)]
        c16 = c_ref[:, block_of(g)]
        for slot, at, total in (
            (0, PAIRS + g, db[...] + dot(ds, c16, 0, 0)),
            (1, PAIRS + GROUPS + g, dc[...] + dot(ds, b16, 1, 0)),
        ):
            mixed = mixed_ref[:, block_of(at)]
            conv_back(at, slot, mixed, sigmoid(mixed), total)
        return 0

    lax.fori_loop(0, GROUPS, group, 0)

    upper = (iota2((T, T), 0) <= iota2((T, T), 1)).astype(F32)
    d_rate = dot(upper, acc[0:T, :], 1, 0, lax.Precision.HIGHEST) - acc[2 * T + 1 : 2 * T + 2, :]
    scale = jnp.exp(head_ref[1:2, :])
    raw = dt_ref[...].astype(F32).T + head_ref[0:1, :]
    d_dt = (acc[T : 2 * T, :] + d_rate * scale) * sigmoid(raw)
    ddt_ref[...] = d_dt.T
    packed_ref[BLOCKS, 0:1, :] = jnp.sum(d_dt, 0, keepdims=True)
    packed_ref[BLOCKS, 1:2, :] = jnp.sum(d_rate * softplus(raw) * scale, 0, keepdims=True)
    packed_ref[BLOCKS, 2:3, :] = acc[2 * T : 2 * T + 1, :]

    def drain(c, _):
        @pl.when(jnp.logical_not(last))
        def _():
            copy(c, out_f, in_f, send_f, recv_f, up).wait_send()

        @pl.when(jnp.logical_not(first))
        def _():
            copy(c, out_b, in_b, send_b, recv_b, down).wait_send()

        return 0

    lax.fori_loop(0, CHUNKS, drain, 0)


def sum_kernel(
    counts, packed_ref, tail_ref, rim_ref, conv_ref, head_ref, end_ref,
    parts, mine, planes, total, rim_in, send_a, recv_a, send_b, recv_b, send_c, recv_c, rim_sem,
):
    n, m = counts
    share = packed_ref.shape[0] // n
    me, plane = lax.axis_index("ctx"), lax.axis_index("fsdp")
    barrier = pltpu.get_barrier_semaphore()
    for r in range(1, n):
        peer = lax.rem(me + r, n)
        pl.semaphore_signal(barrier, inc=1, device_id={"ctx": peer}, device_id_type=MESH)
    for r in range(1, m):
        peer = lax.rem(plane + r, m)
        pl.semaphore_signal(barrier, inc=1, device_id={"fsdp": peer}, device_id_type=MESH)
    pl.semaphore_wait(barrier, n + m - 2)

    def piece(k):
        return pl.ds(k * share, share)

    def rim_copy():
        return pltpu.make_async_remote_copy(
            src_ref=rim_ref, dst_ref=rim_in, send_sem=rim_sem.at[0], recv_sem=rim_sem.at[1],
            device_id={"ctx": jnp.maximum(me - 1, 0)}, device_id_type=MESH,
        )

    def scatter(peer, slot):
        return pltpu.make_async_remote_copy(
            src_ref=packed_ref.at[piece(peer)], dst_ref=parts.at[slot],
            send_sem=send_a.at[peer], recv_sem=recv_a.at[slot],
            device_id={"ctx": peer}, device_id_type=MESH,
        )

    def across(peer, slot):
        return pltpu.make_async_remote_copy(
            src_ref=mine, dst_ref=planes.at[slot],
            send_sem=send_b.at[peer], recv_sem=recv_b.at[slot],
            device_id={"fsdp": peer}, device_id_type=MESH,
        )

    def gather(peer, slot):
        return pltpu.make_async_remote_copy(
            src_ref=total.at[piece(me)], dst_ref=total.at[piece(slot)],
            send_sem=send_c.at[peer], recv_sem=recv_c.at[slot],
            device_id={"ctx": peer}, device_id_type=MESH,
        )

    for r in range(1, n):
        scatter(lax.rem(me + r, n), me).start()

    @pl.when(me > 0)
    def _():
        rim_copy().start()

    parts[me] = packed_ref[piece(me)]
    for r in range(1, n):
        scatter(me, lax.rem(me + r, n)).wait_recv()
    own = parts[0]
    for k in range(1, n):
        own = own + parts[k]
    mine[...] = own
    for r in range(1, m):
        across(lax.rem(plane + r, m), plane).start()
    planes[plane] = own
    for r in range(1, m):
        across(plane, lax.rem(plane + r, m)).wait_recv()
    own = planes[0]
    for k in range(1, m):
        own = own + planes[k]
    total[piece(me)] = own
    for r in range(1, n):
        gather(lax.rem(me + r, n), me).start()

    @pl.when(me == n - 1)
    def _():
        end_ref[...] = tail_ref[...].astype(BF16)

    @pl.when(me < n - 1)
    def _():
        rim_copy().wait_recv()
        shift = TAIL - (CONV_W - 1)
        back = rim_in[...].astype(F32)
        pad = jnp.zeros((shift, CHANNELS), F32)
        moved = jnp.concatenate([pad, back[0 : CONV_W - 1, :]], 0)
        end_ref[...] = (tail_ref[...] + moved).astype(BF16)

    for r in range(1, n):
        gather(me, lax.rem(me + r, n)).wait_recv()
    for i in range(BLOCKS):
        conv_ref[:, i * LANES : (i + 1) * LANES] = total[i, 0 : CONV_W + 1, :]
    head_ref[...] = total[BLOCKS, 0:3, :]
    for r in range(1, n):
        scatter(lax.rem(me + r, n), me).wait_send()
        gather(lax.rem(me + r, n), me).wait_send()
    for r in range(1, m):
        across(lax.rem(plane + r, m), plane).wait_send()

    @pl.when(me > 0)
    def _():
        rim_copy().wait_send()


def vmem(count):
    return [pl.BlockSpec(memory_space=pltpu.VMEM)] * count


def call(kernel, out, scratch, args, limit=56, **params):
    return pl.pallas_call(
        kernel,
        out_shape=[jax.ShapeDtypeStruct(s, d) for s, d in out],
        in_specs=vmem(len(args)),
        out_specs=vmem(len(out)),
        scratch_shapes=scratch,
        compiler_params=pltpu.CompilerParams(vmem_limit_bytes=limit << 20, **params),
    )(*args)


def shifted(block, axis, distance):
    devices = range(lax.axis_size(axis))
    route = [(i - distance, i) for i in devices if i - distance in devices]
    return lax.ppermute(block, axis, route)


def shards(xbc, dt_raw, dy, conv_params, head_params):
    rim_rows = CONV_W - 1
    count = lax.axis_size("ctx")
    x = xbc[0]
    halo = jnp.pad(shifted(x[T - rim_rows :], "ctx", 1), ((8 - rim_rows, 0), (0, 0)))
    base = (x, halo, dt_raw[0], dy[0], conv_params, head_params)
    planes = lax.axis_size("fsdp")
    share = pl.cdiv(BLOCKS + 1, count)
    wide, wide16 = pltpu.VMEM((T, X_WIDTH), F32), pltpu.VMEM((T, X_WIDTH), BF16)
    tall, tall16 = pltpu.VMEM((X_WIDTH, STATE), F32), pltpu.VMEM((X_WIDTH, STATE), BF16)
    small = pltpu.VMEM((T, LANES), F32)
    narrow = pltpu.VMEM((T, GROUPS * STATE), BF16)
    square = pltpu.VMEM((GROUPS, T, T), F32)
    dx, tail, rim, packed, ddt = call(
        functools.partial(main_kernel, count),
        [((T, CHANNELS), BF16), ((TAIL, CHANNELS), F32), ((TAIL, CHANNELS), BF16),
         ((share * count, 8, LANES), F32), ((HEADS, T), F32)],
        [pltpu.VMEM((8 + T, CHANNELS), F32), pltpu.VMEM((2, 16 + T, LANES), F32),
         pltpu.VMEM((T, CHANNELS), F32), wide16, wide, wide, tall, tall,
         tall16, tall16, tall16, tall16, small, small, small, small, narrow, narrow,
         square, square, small, small, pltpu.VMEM((2 * T + 8, HEADS), F32)]
        + [pltpu.SemaphoreType.DMA((CHUNKS,))] * 4,
        base,
        limit=60,
        collective_id=0,
        has_side_effects=True,
    )
    piece = (share, 8, LANES)
    total_conv, total_head, end = call(
        functools.partial(sum_kernel, (count, planes)),
        [((CONV_W + 1, CHANNELS), F32), ((3, HEADS), F32), ((TAIL, CHANNELS), BF16)],
        [pltpu.VMEM((count, *piece), F32), pltpu.VMEM(piece, F32),
         pltpu.VMEM((planes, *piece), F32), pltpu.VMEM((share * count, 8, LANES), F32),
         pltpu.VMEM((TAIL, CHANNELS), BF16)]
        + [pltpu.SemaphoreType.DMA((k,)) for k in (count, count, planes, planes, count, count, 2)],
        (packed, tail, rim),
        collective_id=1,
        has_side_effects=True,
    )
    dx = lax.dynamic_update_slice(dx, end, (T - TAIL, 0))
    return (dx[None], ddt[None], total_conv, total_head)


def solution(mesh):
    return jax.shard_map(
        shards,
        mesh=mesh,
        in_specs=(P("fsdp", "ctx", None), P("fsdp", None, "ctx"), P("fsdp", "ctx", None), P(), P()),
        out_specs=(P("fsdp", "ctx", None), P("fsdp", None, "ctx"), P(), P()),
        check_vma=False,
    )
```

```python
import functools

import jax
import jax.numpy as jnp
from jax import lax
from jax.experimental import pallas as pl
from jax.experimental.pallas import tpu as pltpu
from jax.sharding import PartitionSpec as P

HEADS = 128
HEAD_DIM = 64
STATE = 128
GROUPS = 4
CONV_W = 4
T = 128
LANES = 128
X_WIDTH = HEADS * HEAD_DIM
CHANNELS = X_WIDTH + 2 * GROUPS * STATE
PAIRS = HEADS // 2
PER_GROUP = PAIRS // GROUPS
F32 = jnp.float32
BF16 = jnp.bfloat16
MESH = pl.DeviceIdType.MESH
CHUNKS = 32
CHUNK_HEADS = HEADS // CHUNKS
CHUNK_ROWS = X_WIDTH // CHUNKS
LAG = 3
TAIL = 16
BLOCKS = CHANNELS // LANES


def dot(a, b, ca, cb, precision=None):
    return lax.dot_general(
        a, b, (((ca,), (cb,)), ((), ())), precision=precision, preferred_element_type=F32
    )


def block_of(i):
    return pl.ds(pl.multiple_of(i * LANES, LANES), LANES)


def sigmoid(v):
    return 1.0 / (1.0 + jnp.exp(-v))


def softplus(v):
    z = jnp.exp(-jnp.abs(v))
    small = z * (1.0 - z * (0.5 - z * (1.0 / 3.0 - z * 0.25)))
    return jnp.maximum(v, 0.0) + jnp.where(z < 0.01, small, jnp.log(1.0 + z))


def iota2(shape, dim):
    return lax.broadcasted_iota(jnp.int32, shape, dim)


def wide_pair(ht_ref, h):
    top = jnp.broadcast_to(ht_ref[pl.ds(h, 1), :], (HEAD_DIM, T))
    low = jnp.broadcast_to(ht_ref[pl.ds(h + 1, 1), :], (HEAD_DIM, T))
    return jnp.concatenate([top, low], axis=0).T


def main_kernel(
    count,
    xbc_ref, halo_ref, dt_ref, dy_ref, conv_ref, head_ref,
    dx_ref, tail_ref, rim_ref, packed_ref, ddt_ref,
    ext, dms, mixed_ref, xd_ref, y_ref, dxd_ref, leave_ref, pull_ref,
    out_f, out_b, in_f, in_b, fade_ref, run_ref, step_ref, skip_ref, b_ref, c_ref,
    scores, dscores, db, dc, acc, send_f, recv_f, send_b, recv_b,
):
    me = lax.axis_index("ctx")
    barrier = pltpu.get_barrier_semaphore()
    first, last = me == 0, me == count - 1
    for peer in (lax.rem(me + 1, count), lax.rem(me + count - 1, count)):
        pl.semaphore_signal(barrier, inc=1, device_id={"ctx": peer}, device_id_type=MESH)

    step_th = softplus(dt_ref[...].astype(F32).T + head_ref[0:1, :])
    rate_th = step_th * jnp.exp(head_ref[1:2, :])
    lower = (iota2((T, T), 0) >= iota2((T, T), 1)).astype(F32)
    run_ht = dot(lower, rate_th, 1, 0, lax.Precision.HIGHEST).T
    run_ref[...] = run_ht
    step_ref[...] = step_th.T
    fade_ref[...] = jnp.broadcast_to(jnp.exp(-run_ht[:, T - 1 : T]), (HEADS, LANES))
    skip_ref[...] = jnp.broadcast_to(head_ref[2:3, :], (LANES, HEADS)).T
    acc[...] = jnp.zeros_like(acc)
    packed_ref[...] = jnp.zeros_like(packed_ref)
    dscores[...] = jnp.zeros_like(dscores)
    for slot in range(2):
        dms[slot, 0:8, :] = jnp.zeros((8, LANES), F32)
        dms[slot, 8 + T : 16 + T, :] = jnp.zeros((8, LANES), F32)
    causal = iota2((T, T), 0) >= iota2((T, T), 1)
    left = iota2((T, LANES), 1) < HEAD_DIM
    zero = jnp.zeros((T, LANES), BF16)

    def split(v):
        return jnp.concatenate([jnp.where(left, v, zero), jnp.where(left, zero, v)], 0)

    def convolve(i):
        cols = block_of(i)
        ext[0:8, cols] = halo_ref[:, cols].astype(F32)
        ext[8 : 8 + T, cols] = xbc_ref[:, cols].astype(F32)
        mixed = conv_ref[CONV_W : CONV_W + 1, cols] + conv_ref[0:1, cols] * ext[5 : 5 + T, cols]
        for j in range(1, CONV_W):
            mixed = mixed + conv_ref[j : j + 1, cols] * ext[5 + j : 5 + j + T, cols]
        mixed_ref[:, cols] = mixed
        return mixed * sigmoid(mixed)

    def bc(g, _):
        b16 = convolve(PAIRS + g).astype(BF16)
        c16 = convolve(PAIRS + GROUPS + g).astype(BF16)
        b_ref[:, block_of(g)] = b16
        c_ref[:, block_of(g)] = c16
        scores[g] = dot(c16, b16, 1, 1)
        return 0

    lax.fori_loop(0, GROUPS, bc, 0)

    def states(i):
        g = i // PER_GROUP
        x = convolve(i)
        run = wide_pair(run_ref, 2 * i)
        xd = (x * wide_pair(step_ref, 2 * i)).astype(BF16)
        xd_ref[:, block_of(i)] = xd
        tail = (xd.astype(F32) * jnp.exp(run - run[T - 1 : T, :])).astype(BF16)
        out = (jnp.exp(-run) * dy_ref[:, block_of(i)].astype(F32)).astype(BF16)
        leave_ref[block_of(i), :] = dot(tail, b_ref[:, block_of(g)], 0, 0)
        pull_ref[block_of(i), :] = dot(out, c_ref[:, block_of(g)], 0, 0)

    pl.semaphore_wait(barrier, 2)

    def rows_of(c):
        return pl.ds(pl.multiple_of(c * CHUNK_ROWS, CHUNK_ROWS), CHUNK_ROWS)

    def copy(c, src, dst, send, recv, peer):
        return pltpu.make_async_remote_copy(
            src_ref=src.at[rows_of(c)], dst_ref=dst.at[rows_of(c)],
            send_sem=send.at[c], recv_sem=recv.at[c],
            device_id={"ctx": peer}, device_id_type=MESH,
        )

    def handle(c, own, src, dst, send, recv, peer, begins, ends):
        @pl.when(begins)
        def _():
            dst[rows_of(c), :] = jnp.zeros((CHUNK_ROWS, LANES), BF16)

        @pl.when(jnp.logical_not(begins))
        def _():
            copy(c, src, dst, send, recv, peer).wait_recv()

        @pl.when(jnp.logical_not(ends))
        def _():
            for k in range(CHUNK_HEADS):
                rows = pl.ds(pl.multiple_of(c * CHUNK_ROWS + k * HEAD_DIM, HEAD_DIM), HEAD_DIM)
                fade = fade_ref[pl.ds(c * CHUNK_HEADS + k, 1), :]
                src[rows, :] = (fade * dst[rows, :].astype(F32) + own[rows, :]).astype(BF16)
            copy(c, src, dst, send, recv, peer).start()

    up = jnp.minimum(me + 1, count - 1)
    down = jnp.maximum(me - 1, 0)
    ticks = CHUNKS + (count - 1) * LAG
    later_ticks = ticks - CHUNKS
    load = pl.cdiv(PAIRS, later_ticks)
    per_chunk = PAIRS // CHUNKS

    def inner(i):
        h = 2 * i
        g = i // PER_GROUP
        cols = block_of(i)
        fades = []
        for k in range(2):
            row = jnp.broadcast_to(run_ref[pl.ds(h + k, 1), :], (T, T))
            fades.append(jnp.exp(jnp.where(causal, row - row.T, -1e30)))
        dy16 = dy_ref[:, cols]
        bd_x = split(xd_ref[:, cols])
        sc = scores[g]
        w = [(sc * f).astype(BF16) for f in fades]
        y_ref[:, cols] = dot(jnp.concatenate(w, 1), bd_x, 1, 0)
        dxd_ref[:, cols] = dot(jnp.concatenate(w, 0), split(dy16), 0, 0)
        pairwise = dot(dy16, bd_x, 1, 1)
        dscores[g] += pairwise[:, :T] * fades[0] + pairwise[:, T:] * fades[1]

    def tick(v, _):
        @pl.when(v < CHUNKS)
        def _():
            for k in range(per_chunk):
                states(v * per_chunk + k)

        c = v - me * LAG

        @pl.when(jnp.logical_and(c >= 0, c < CHUNKS))
        def _():
            handle(c, leave_ref, out_f, in_f, send_f, recv_f, up, first, last)

        d = v - (count - 1 - me) * LAG

        @pl.when(jnp.logical_and(d >= 0, d < CHUNKS))
        def _():
            handle(d, pull_ref, out_b, in_b, send_b, recv_b, down, last, first)

        w = v - CHUNKS

        @pl.when(jnp.logical_and(w >= 0, (w + 1) * load <= PAIRS))
        def _():
            for k in range(load):
                inner(w * load + k)

        return 0

    lax.fori_loop(0, ticks, tick, 0)
    for i in range(PAIRS // load * load, PAIRS):
        inner(i)

    def conv_back(i, slot, mixed, sig, dact):
        cols = block_of(i)
        dm = dact * (sig * (1.0 + mixed * (1.0 - sig)))
        dms[slot, 8 : 8 + T, :] = dm
        taps = [conv_ref[j : j + 1, cols] for j in range(CONV_W)]
        own = taps[3] * dm
        rim = taps[0] * dms[slot, 8:16, :]
        for j in range(3):
            own = own + taps[j] * dms[slot, 11 - j : 11 - j + T, :]
        for j in range(1, 3):
            rim = rim + taps[j] * dms[slot, 8 - j : 16 - j, :]
        dx_ref[:, cols] = own.astype(BF16)
        tail_ref[:, cols] = own[T - TAIL :, :]
        rim_ref[:, cols] = jnp.concatenate([rim, jnp.zeros_like(rim)], 0).astype(BF16)
        for j in range(CONV_W):
            packed_ref[i, j : j + 1, :] = jnp.sum(
                dm * ext[5 + j : 5 + j + T, cols], 0, keepdims=True
            )
        packed_ref[i, CONV_W : CONV_W + 1, :] = jnp.sum(dm, 0, keepdims=True)

    def pair(i, g, slot):
        h = 2 * i
        cols = block_of(i)
        mixed = mixed_ref[:, cols]
        sig = sigmoid(mixed)
        x = mixed * sig
        dy = dy_ref[:, cols].astype(F32)
        step = wide_pair(step_ref, h)
        run = wide_pair(run_ref, h)
        xd = xd_ref[:, cols].astype(F32)
        e_tail = jnp.exp(run - run[T - 1 : T, :])
        e_head = jnp.exp(-run)
        enter = in_f[cols, :]
        later = in_b[cols, :]
        y = y_ref[:, cols] + e_head * dot(c_ref[:, block_of(g)], enter, 1, 1)
        from_tail = e_tail * dot(b_ref[:, block_of(g)], later, 1, 1)
        dxd = dxd_ref[:, cols] + from_tail
        dc[...] += dot((e_head * dy).astype(BF16), enter, 1, 0)
        db[...] += dot((xd * e_tail).astype(BF16), later, 1, 0)
        skip = jnp.where(left[0:1, :], skip_ref[pl.ds(h, 1), :], skip_ref[pl.ds(h + 1, 1), :])
        conv_back(i, slot, mixed, sig, step * dxd + skip * dy)
        both = (enter.astype(F32) * later.astype(F32)).astype(BF16)
        passed = dot(jnp.ones((8, STATE), BF16), both, 1, 1)
        sub = iota2((8, LANES), 0)
        rows = jnp.where(sub == 0, jnp.sum(dy * x, 0, keepdims=True), 0.0)
        rows = rows + jnp.where(
            sub == 1,
            jnp.sum(xd * from_tail, 0, keepdims=True) + e_head[T - 1 : T, :] * passed[0:1, :],
            0.0,
        )
        value = jnp.concatenate([xd * dxd - dy * y, x * dxd, rows], 0)
        high = value.astype(BF16)
        low = (value - high.astype(F32)).astype(BF16)
        pick = (iota2((LANES, HEADS), 1) == h + iota2((LANES, HEADS), 0) // HEAD_DIM).astype(BF16)
        acc[...] += dot(
            jnp.concatenate([high, low], 1), jnp.concatenate([pick, pick], 0), 1, 0
        )

    def group(g, _):
        db[...] = jnp.zeros_like(db)
        dc[...] = jnp.zeros_like(dc)

        def two(k, _):
            pair(g * PER_GROUP + 2 * k, g, 0)
            pair(g * PER_GROUP + 2 * k + 1, g, 1)
            return 0

        lax.fori_loop(0, PER_GROUP // 2, two, 0)
        ds = dscores[g].astype(BF16)
        b16 = b_ref[:, block_of(g)]
        c16 = c_ref[:, block_of(g)]
        for slot, at, total in (
            (0, PAIRS + g, db[...] + dot(ds, c16, 0, 0)),
            (1, PAIRS + GROUPS + g, dc[...] + dot(ds, b16, 1, 0)),
        ):
            mixed = mixed_ref[:, block_of(at)]
            conv_back(at, slot, mixed, sigmoid(mixed), total)
        return 0

    lax.fori_loop(0, GROUPS, group, 0)

    upper = (iota2((T, T), 0) <= iota2((T, T), 1)).astype(F32)
    d_rate = dot(upper, acc[0:T, :], 1, 0, lax.Precision.HIGHEST) - acc[2 * T + 1 : 2 * T + 2, :]
    scale = jnp.exp(head_ref[1:2, :])
    raw = dt_ref[...].astype(F32).T + head_ref[0:1, :]
    d_dt = (acc[T : 2 * T, :] + d_rate * scale) * sigmoid(raw)
    ddt_ref[...] = d_dt.T
    packed_ref[BLOCKS, 0:1, :] = jnp.sum(d_dt, 0, keepdims=True)
    packed_ref[BLOCKS, 1:2, :] = jnp.sum(d_rate * softplus(raw) * scale, 0, keepdims=True)
    packed_ref[BLOCKS, 2:3, :] = acc[2 * T : 2 * T + 1, :]

    def drain(c, _):
        @pl.when(jnp.logical_not(last))
        def _():
            copy(c, out_f, in_f, send_f, recv_f, up).wait_send()

        @pl.when(jnp.logical_not(first))
        def _():
            copy(c, out_b, in_b, send_b, recv_b, down).wait_send()

        return 0

    lax.fori_loop(0, CHUNKS, drain, 0)


def sum_kernel(
    counts, packed_ref, tail_ref, rim_ref, conv_ref, head_ref, end_ref,
    parts, mine, planes, total, rim_in, send_a, recv_a, send_b, recv_b, send_c, recv_c, rim_sem,
):
    n, m = counts
    share = packed_ref.shape[0] // n
    me, plane = lax.axis_index("ctx"), lax.axis_index("fsdp")
    barrier = pltpu.get_barrier_semaphore()
    for r in range(1, n):
        peer = lax.rem(me + r, n)
        pl.semaphore_signal(barrier, inc=1, device_id={"ctx": peer}, device_id_type=MESH)
    for r in range(1, m):
        peer = lax.rem(plane + r, m)
        pl.semaphore_signal(barrier, inc=1, device_id={"fsdp": peer}, device_id_type=MESH)
    pl.semaphore_wait(barrier, n + m - 2)

    def piece(k):
        return pl.ds(k * share, share)

    def rim_copy():
        return pltpu.make_async_remote_copy(
            src_ref=rim_ref, dst_ref=rim_in, send_sem=rim_sem.at[0], recv_sem=rim_sem.at[1],
            device_id={"ctx": jnp.maximum(me - 1, 0)}, device_id_type=MESH,
        )

    def scatter(peer, slot):
        return pltpu.make_async_remote_copy(
            src_ref=packed_ref.at[piece(peer)], dst_ref=parts.at[slot],
            send_sem=send_a.at[peer], recv_sem=recv_a.at[slot],
            device_id={"ctx": peer}, device_id_type=MESH,
        )

    def across(peer, slot):
        return pltpu.make_async_remote_copy(
            src_ref=mine, dst_ref=planes.at[slot],
            send_sem=send_b.at[peer], recv_sem=recv_b.at[slot],
            device_id={"fsdp": peer}, device_id_type=MESH,
        )

    def gather(peer, slot):
        return pltpu.make_async_remote_copy(
            src_ref=total.at[piece(me)], dst_ref=total.at[piece(slot)],
            send_sem=send_c.at[peer], recv_sem=recv_c.at[slot],
            device_id={"ctx": peer}, device_id_type=MESH,
        )

    for r in range(1, n):
        scatter(lax.rem(me + r, n), me).start()

    @pl.when(me > 0)
    def _():
        rim_copy().start()

    parts[me] = packed_ref[piece(me)]
    for r in range(1, n):
        scatter(me, lax.rem(me + r, n)).wait_recv()
    own = parts[0]
    for k in range(1, n):
        own = own + parts[k]
    mine[...] = own
    for r in range(1, m):
        across(lax.rem(plane + r, m), plane).start()
    planes[plane] = own
    for r in range(1, m):
        across(plane, lax.rem(plane + r, m)).wait_recv()
    own = planes[0]
    for k in range(1, m):
        own = own + planes[k]
    total[piece(me)] = own
    for r in range(1, n):
        gather(lax.rem(me + r, n), me).start()

    @pl.when(me == n - 1)
    def _():
        end_ref[...] = tail_ref[...].astype(BF16)

    @pl.when(me < n - 1)
    def _():
        rim_copy().wait_recv()
        shift = TAIL - (CONV_W - 1)
        back = rim_in[...].astype(F32)
        pad = jnp.zeros((shift, CHANNELS), F32)
        moved = jnp.concatenate([pad, back[0 : CONV_W - 1, :]], 0)
        end_ref[...] = (tail_ref[...] + moved).astype(BF16)

    for r in range(1, n):
        gather(me, lax.rem(me + r, n)).wait_recv()
    for i in range(BLOCKS):
        conv_ref[:, i * LANES : (i + 1) * LANES] = total[i, 0 : CONV_W + 1, :]
    head_ref[...] = total[BLOCKS, 0:3, :]
    for r in range(1, n):
        scatter(lax.rem(me + r, n), me).wait_send()
        gather(lax.rem(me + r, n), me).wait_send()
    for r in range(1, m):
        across(lax.rem(plane + r, m), plane).wait_send()

    @pl.when(me > 0)
    def _():
        rim_copy().wait_send()


def vmem(count):
    return [pl.BlockSpec(memory_space=pltpu.VMEM)] * count


def call(kernel, out, scratch, args, limit=56, **params):
    return pl.pallas_call(
        kernel,
        out_shape=[jax.ShapeDtypeStruct(s, d) for s, d in out],
        in_specs=vmem(len(args)),
        out_specs=vmem(len(out)),
        scratch_shapes=scratch,
        compiler_params=pltpu.CompilerParams(vmem_limit_bytes=limit << 20, **params),
    )(*args)


def shifted(block, axis, distance):
    devices = range(lax.axis_size(axis))
    route = [(i - distance, i) for i in devices if i - distance in devices]
    return lax.ppermute(block, axis, route)


def shards(xbc, dt_raw, dy, conv_params, head_params):
    rim_rows = CONV_W - 1
    count = lax.axis_size("ctx")
    x = xbc[0]
    halo = jnp.pad(shifted(x[T - rim_rows :], "ctx", 1), ((8 - rim_rows, 0), (0, 0)))
    base = (x, halo, dt_raw[0], dy[0], conv_params, head_params)
    planes = lax.axis_size("fsdp")
    share = pl.cdiv(BLOCKS + 1, count)
    wide, wide16 = pltpu.VMEM((T, X_WIDTH), F32), pltpu.VMEM((T, X_WIDTH), BF16)
    tall, tall16 = pltpu.VMEM((X_WIDTH, STATE), F32), pltpu.VMEM((X_WIDTH, STATE), BF16)
    small = pltpu.VMEM((T, LANES), F32)
    narrow = pltpu.VMEM((T, GROUPS * STATE), BF16)
    square = pltpu.VMEM((GROUPS, T, T), F32)
    dx, tail, rim, packed, ddt = call(
        functools.partial(main_kernel, count),
        [((T, CHANNELS), BF16), ((TAIL, CHANNELS), F32), ((TAIL, CHANNELS), BF16),
         ((share * count, 8, LANES), F32), ((HEADS, T), F32)],
        [pltpu.VMEM((8 + T, CHANNELS), F32), pltpu.VMEM((2, 16 + T, LANES), F32),
         pltpu.VMEM((T, CHANNELS), F32), wide16, wide, wide, tall, tall,
         tall16, tall16, tall16, tall16, small, small, small, small, narrow, narrow,
         square, square, small, small, pltpu.VMEM((2 * T + 8, HEADS), F32)]
        + [pltpu.SemaphoreType.DMA((CHUNKS,))] * 4,
        base,
        limit=60,
        collective_id=0,
        has_side_effects=True,
    )
    piece = (share, 8, LANES)
    total_conv, total_head, end = call(
        functools.partial(sum_kernel, (count, planes)),
        [((CONV_W + 1, CHANNELS), F32), ((3, HEADS), F32), ((TAIL, CHANNELS), BF16)],
        [pltpu.VMEM((count, *piece), F32), pltpu.VMEM(piece, F32),
         pltpu.VMEM((planes, *piece), F32), pltpu.VMEM((share * count, 8, LANES), F32),
         pltpu.VMEM((TAIL, CHANNELS), BF16)]
        + [pltpu.SemaphoreType.DMA((k,)) for k in (count, count, planes, planes, count, count, 2)],
        (packed, tail, rim),
        collective_id=1,
        has_side_effects=True,
    )
    dx = jnp.concatenate([dx[: T - TAIL], end], axis=0)
    return (dx[None], ddt[None], total_conv, total_head)


def solution(mesh):
    return jax.shard_map(
        shards,
        mesh=mesh,
        in_specs=(P("fsdp", "ctx", None), P("fsdp", None, "ctx"), P("fsdp", "ctx", None), P(), P()),
        out_specs=(P("fsdp", "ctx", None), P("fsdp", None, "ctx"), P(), P()),
        check_vma=False,
    )
```
